256 devices in a mesh: sys: 16 (over y_lo, x, core), atom: 16 (over z, y_hi).
Axes of the slice: x: 4, y: 4 (y_hi: 2, y_lo: 2; y = y_hi * 2 + y_lo), z: 8, core: 2. Of those that a mesh axis runs over, the one named last changes fastest.
Arguments:
- atoms: bfloat16 [65536, 512], P(('sys', 'atom')), parts along dimension 0, may hold values from -70 to 70
- neighbours: int32 [65536, 32], P(('sys', 'atom')), parts along dimension 0, may hold values from 0 to 4095, as said below
- counts: int32 [65536], P(('sys', 'atom')), parts along dimension 0, may hold values from 1 to 32
- envelope: float32 [65536, 32], P(('sys', 'atom')), parts along dimension 0, may hold values from 0.1 to 1
- w_self: bfloat16 [512, 512], replicated, may hold values from -0.25 to 0.25
- w_other: bfloat16 [512, 512], replicated, may hold values from -0.25 to 0.25
- w_edge: bfloat16 [512, 512], replicated, may hold values from -0.25 to 0.25
- edge_gain: float32 [512], replicated, may hold values from 0.25 to 1.75
- w_query: bfloat16 [512, 512], replicated, may hold values from -0.25 to 0.25
- w_key: bfloat16 [512, 512], replicated, may hold values from -0.25 to 0.25
- w_value: bfloat16 [512, 512], replicated, may hold values from -0.25 to 0.25
- w_out: bfloat16 [512, 512], replicated, may hold values from -0.25 to 0.25
Outputs:
- updated: bfloat16 [65536, 512], P(('sys', 'atom')), parts along dimension 0
The draws below stay inside these ranges and needn't reach their ends.
There are 16 independent parts, one for each index of `sys`. The reference program is written for one: setup_inputs(seed, part) draws one part's arguments, and reference() takes and returns one part's arrays. A program takes and returns all parts, laid end to end along the dimension named above; an argument that names none is the same for every part. Nothing has to cross between parts.
Inputs may be any that keep to these rules, and one draw needn't show every extreme that they name: `neighbours`: for slot k < counts[i] of atom i the neighbour j satisfies (j - i) mod 4096 in 1 .. 128 or in 3968 .. 4095, and both offsets + 128 and - 128 occur; slots k >= counts[i] hold i itself.
All inputs are finite; a program needn't handle non-finite values.
Results may differ from the reference program's by a relative error of at most 0.038.
Values may be sent and summed in bfloat16 or wider, within the bound.
No kernel may reach another device: no remote copies, remote signals or barrier semaphores. Data moves between devices by JAX's collectives and lax.ppermute only.
A program may use at most 64 MiB of HBM per device.

```python
import math
import jax
import jax.numpy as jnp
from jax import lax

D = 512
HEADS = 8
K_NBR = 32
HEAD_DIM = 64
ATOMS = 4096
REACH = 128


def counts_from(key):
    values = jax.random.randint(jax.random.fold_in(key, 11), (ATOMS,), 1, K_NBR + 1).astype(jnp.int32)
    values = values.at[0].set(K_NBR)
    values = values.at[1].set(1)
    return values


def draw_counts(key, part):
    return counts_from(key)


def draw_neighbours(key, part):
    valid_counts = counts_from(key)
    distance = jax.random.randint(jax.random.fold_in(key, 23), (ATOMS, K_NBR), 1, REACH + 1).astype(jnp.int32)
    direction = jax.random.randint(jax.random.fold_in(key, 37), (ATOMS, K_NBR), 0, 2).astype(jnp.int32) * 2 - 1
    offset = distance * direction
    offset = offset.at[0, 0].set(REACH)
    offset = offset.at[1, 0].set(-REACH)
    own_index = jnp.arange(ATOMS, dtype=jnp.int32)[:, None]
    target = jnp.mod(own_index + offset, ATOMS).astype(jnp.int32)
    slot_ids = jnp.arange(K_NBR, dtype=jnp.int32)[None, :]
    return jnp.where(slot_ids < valid_counts[:, None], target, own_index).astype(jnp.int32)


def draw_atoms(key, part):
    values = jax.random.truncated_normal(jax.random.fold_in(key, 41), -5.0, 5.0, (ATOMS, D), jnp.float32)
    return values.astype(jnp.bfloat16)


def shard_levels(key, extent, pieces, least, top_value):
    loudness = 1.0
    for position, parts in pieces:
        steps = jax.random.uniform(jax.random.fold_in(jax.random.fold_in(key, 6), position), (parts,), jnp.float32, least / len(pieces), top_value / len(pieces))
        loudness = loudness * jnp.repeat(jnp.exp(steps), extent[position] // parts).reshape((-1,) + (1,) * (len(extent) - 1 - position))
    return loudness


def centred(stream_key, extent, scale, limit, kind=jnp.bfloat16):
    return jnp.clip(scale * jax.random.normal(stream_key, extent, jnp.float32), -limit, limit).astype(kind)


def setup_inputs(seed: int = 0, part: int = 0) -> dict:
    splits = jax.random.split(jax.random.key(seed), 13)
    own_keys = jax.random.split(jax.random.fold_in(splits[12], part), 13)
    return {
        "atoms": draw_atoms(jax.random.fold_in(jax.random.fold_in(splits[12], part), 71), part),
        "neighbours": draw_neighbours(jax.random.fold_in(jax.random.fold_in(splits[12], part), 71), part),
        "counts": draw_counts(jax.random.fold_in(jax.random.fold_in(splits[12], part), 71), part),
        "envelope": jnp.clip(0.1 + 0.9 * jax.random.uniform(own_keys[3], (ATOMS, K_NBR), jnp.float32) ** shard_levels(own_keys[3], (ATOMS, K_NBR), ((0, 16),), -0.2, 0.2), 0.1, 1.0),
        "w_self": centred(splits[4], (D, D), D ** -0.5, 0.25),
        "w_other": centred(splits[5], (D, D), D ** -0.5, 0.25),
        "w_edge": centred(splits[6], (D, D), D ** -0.5, 0.25),
        "edge_gain": jnp.clip(1.0 + 0.15 * jax.random.normal(splits[7], (D,), jnp.float32), 0.25, 1.75),
        "w_query": centred(splits[8], (D, D), D ** -0.5, 0.25),
        "w_key": centred(splits[9], (D, D), D ** -0.5, 0.25),
        "w_value": centred(splits[10], (D, D), D ** -0.5, 0.25),
        "w_out": centred(splits[11], (D, D), D ** -0.5, 0.25),
    }


def reference(atoms, neighbours, counts, envelope, w_self, w_other, w_edge, edge_gain, w_query, w_key, w_value, w_out):
    self_part = jnp.dot(atoms, w_self, preferred_element_type=jnp.float32)
    other_rows = jnp.dot(atoms, w_other, preferred_element_type=jnp.float32).astype(jnp.bfloat16)
    slot_ids = jnp.arange(K_NBR, dtype=jnp.int32)
    edge_weight = jnp.where(slot_ids[None, :] < counts[:, None], envelope, jnp.float32(0.0))
    edge_block = math.gcd(ATOMS, 256)
    block_count = ATOMS // edge_block
    edge_float = w_edge.astype(jnp.float32)

    def edge_step(packed):
        self_block, index_block, weight_block = packed
        picked = jnp.take(other_rows, index_block, axis=0).astype(jnp.float32)
        pre_act = jax.nn.silu(self_block[:, None, :] + picked).astype(jnp.bfloat16)
        message = jax.nn.silu(jnp.einsum('rkd,de->rke', pre_act.astype(jnp.float32), edge_float))
        return jnp.einsum('rk,rkd->rd', weight_block, message)
    edge_sum = lax.map(edge_step, (self_part.reshape(block_count, edge_block, D), neighbours.reshape(block_count, edge_block, K_NBR), edge_weight.reshape(block_count, edge_block, K_NBR))).reshape(ATOMS, D)
    mean_square = lax.optimization_barrier(jnp.mean(edge_sum * edge_sum, axis=1, keepdims=True))
    normed = edge_gain[None, :] * edge_sum / jnp.sqrt(mean_square + 1e-05)
    mixed_rows = (atoms.astype(jnp.float32) + normed).astype(jnp.bfloat16)
    queries = jnp.dot(mixed_rows, w_query, preferred_element_type=jnp.float32).astype(jnp.bfloat16)
    key_rows = jnp.dot(mixed_rows, w_key, preferred_element_type=jnp.float32).astype(jnp.bfloat16)
    value_rows = jnp.dot(mixed_rows, w_value, preferred_element_type=jnp.float32).astype(jnp.bfloat16)
    key_heads = key_rows.reshape(ATOMS, HEADS, HEAD_DIM).astype(jnp.float32)
    value_heads = value_rows.reshape(ATOMS, HEADS, HEAD_DIM).astype(jnp.float32)
    query_block = math.gcd(ATOMS, 512)
    query_count = ATOMS // query_block
    score_scale = 1.0 / math.sqrt(HEAD_DIM)

    def attend_step(query_rows):
        query_heads = query_rows.reshape(query_block, HEADS, HEAD_DIM).astype(jnp.float32)
        scores = jnp.einsum('qhd,khd->qhk', query_heads, key_heads) * score_scale
        top = lax.optimization_barrier(jnp.max(scores, axis=2, keepdims=True))
        weights = jnp.exp(scores - top)
        denominator = lax.optimization_barrier(jnp.sum(weights, axis=2))
        weighted = jnp.einsum('qhk,khd->qhd', weights.astype(jnp.bfloat16).astype(jnp.float32), value_heads)
        return (weighted / denominator[:, :, None]).reshape(query_block, D)
    attended = lax.map(attend_step, queries.reshape(query_count, query_block, D)).reshape(ATOMS, D).astype(jnp.bfloat16)
    result = mixed_rows.astype(jnp.float32) + jnp.dot(attended, w_out, preferred_element_type=jnp.float32)
    return result.astype(jnp.bfloat16)
```

```python
import functools
import math

import jax
import jax.numpy as jnp
from jax import lax
from jax.experimental import pallas as pl
from jax.experimental.pallas import tpu as pltpu
from jax.sharding import PartitionSpec as P

HEADS = 8
HEAD_DIM = 64

NT = (((1,), (1,)), ((), ()))
TN = (((0,), (0,)), ((), ()))


def mm(a, b, dims=(((1,), (0,)), ((), ()))):
    return lax.dot_general(a, b, dims, preferred_element_type=jnp.float32)


def silu(x):
    h = 0.5 * x
    return h + h * jnp.tanh(h)


def prep_kernel(own, w_self, w_other, w_edge, self_t, other_t, edge_t):
    self_t[...] = mm(w_self[...].T, own[...], NT)
    other_t[...] = mm(w_other[...].T, own[...], NT).astype(jnp.bfloat16)
    edge_t[...] = w_edge[...].T


def edge_kernel(own, before, after, idx_t, ew_t, self_t, other_own, w_other, edge_t, gain, mixed, table, acc):
    rows = own.shape[0]
    half = rows // 2
    slots = idx_t.shape[0]
    w_t = w_other[...].T
    table[:, :half] = mm(w_t, before[...], NT).astype(jnp.bfloat16)
    table[:, half : half + rows] = other_own[...]
    table[:, half + rows :] = mm(w_t, after[...], NT).astype(jnp.bfloat16)
    acc[...] = jnp.zeros_like(acc)
    span = table.shape[1]

    def step(k, carry):
        hot = lax.broadcasted_iota(jnp.int32, (span, rows), 0) == idx_t[pl.ds(k, 1), :]
        picked = mm(table[...], jnp.where(hot, 1.0, 0.0).astype(jnp.bfloat16))
        pre = silu(self_t[...] + picked).astype(jnp.bfloat16)
        message = silu(mm(edge_t[...], pre))
        acc[...] += ew_t[pl.ds(k, 1), :] * message
        return carry

    lax.fori_loop(0, slots, step, 0, unroll=2)
    total = acc[...]
    mean_square = jnp.mean(total * total, axis=0, keepdims=True)
    normed = total * lax.rsqrt(mean_square + 1e-05)
    mixed[...] = (own[...].astype(jnp.float32) + gain[...] * normed.T).astype(jnp.bfloat16)


def query_kernel(own, w_query, w_value, query, value_t):
    scale = math.log2(math.e) / math.sqrt(HEAD_DIM)
    q_t = (mm(w_query[...].T, own[...], NT) * scale).astype(jnp.bfloat16)
    zero = jnp.zeros((HEAD_DIM, q_t.shape[1]), jnp.bfloat16)
    for h in range(HEADS):
        lo = h * HEAD_DIM
        mine = (h % 2) * HEAD_DIM
        query[h, mine : mine + HEAD_DIM, :] = q_t[lo : lo + HEAD_DIM]
        query[h, HEAD_DIM - mine : 2 * HEAD_DIM - mine, :] = zero
    value_t[...] = w_value[...].T


def attend_kernel(shards, first, last, *refs):
    xs, refs = refs[:shards], refs[shards:]
    query, w_key, value_w, refs = refs[0], refs[1], refs[2], refs[3:]
    if not first:
        state_in, sums_in, refs = refs[0], refs[1], refs[2:]
    if last:
        own, w_out, out, refs = refs[0], refs[1], refs[2], refs[3:]
        state, sums, refs = refs[0], refs[1], refs[2:]
    else:
        state, sums, refs = refs[0], refs[1], refs[2:]
    stack, keys, values = refs
    for i, x in enumerate(xs):
        stack[i] = x[...]
    if first:
        state[...] = jnp.zeros_like(state)
        sums[0:HEADS] = jnp.full((HEADS, sums.shape[1]), -1e30, jnp.float32)
        sums[HEADS:] = jnp.zeros((HEADS, sums.shape[1]), jnp.float32)
    else:
        state[...] = state_in[...]
        sums[...] = sums_in[...]

    def step(i, carry):
        x = stack[i]
        keys[...] = mm(x, w_key[...]).astype(jnp.bfloat16)
        values[...] = mm(value_w[...], x, NT).astype(jnp.bfloat16)
        for h in range(HEADS):
            pair = (h // 2) * 2 * HEAD_DIM
            rows = pl.ds(h * HEAD_DIM, HEAD_DIM)
            scores = mm(keys[:, pair : pair + 2 * HEAD_DIM], query[h])
            old = sums[h : h + 1]
            top = jnp.maximum(old, jnp.max(scores, axis=0, keepdims=True))
            factor = jnp.exp2(old - top)
            weights = jnp.exp2(scores - top)
            sums[h : h + 1] = top
            sums[HEADS + h : HEADS + h + 1] = factor * sums[HEADS + h : HEADS + h + 1] + jnp.sum(
                weights, axis=0, keepdims=True
            )
            state[rows, :] = factor * state[rows, :] + mm(values[rows, :], weights.astype(jnp.bfloat16))
        return carry

    lax.fori_loop(0, shards, step, 0)
    if last:
        for h in range(HEADS):
            rows = pl.ds(h * HEAD_DIM, HEAD_DIM)
            state[rows, :] = state[rows, :] / sums[HEADS + h : HEADS + h + 1]
        attended = state[...].T.astype(jnp.bfloat16)
        out[...] = (own[...].astype(jnp.float32) + mm(attended, w_out[...])).astype(jnp.bfloat16)


def call(body, out_shape, scratch=(), cost=None, name=None):
    flops, trans = cost
    return pl.pallas_call(
        body,
        out_shape=out_shape,
        scratch_shapes=list(scratch),
        cost_estimate=pl.CostEstimate(flops=flops, transcendentals=trans, bytes_accessed=2**21),
        compiler_params=pltpu.CompilerParams(vmem_limit_bytes=40 * 2**20),
        name=name,
    )


def bf16(*shape):
    return jax.ShapeDtypeStruct(shape, jnp.bfloat16)


def f32(*shape):
    return jax.ShapeDtypeStruct(shape, jnp.float32)


def attend(xs, query, w_key, value_w, carry, tail, name):
    rows, width = xs[0].shape
    first, last = carry is None, tail is not None
    shards = len(xs)
    scratch = [
        pltpu.VMEM((shards, rows, width), jnp.bfloat16),
        pltpu.VMEM((rows, width), jnp.bfloat16),
        pltpu.VMEM((width, rows), jnp.bfloat16),
    ]
    if last:
        out_shape = bf16(rows, width)
        scratch = [pltpu.VMEM((width, rows), jnp.float32), pltpu.VMEM((2 * HEADS, rows), jnp.float32)] + scratch
    else:
        out_shape = (f32(width, rows), f32(2 * HEADS, rows))
    cost = (shards * 4 * rows * width * width * 2, shards * HEADS * rows * rows)
    body = functools.partial(attend_kernel, shards, first, last)
    args = list(xs) + [query, w_key, value_w] + ([] if first else list(carry)) + (list(tail) if last else [])
    return call(body, out_shape, scratch, cost, name)(*args)


def per_device(
    atoms, neighbours, counts, envelope, w_self, w_other, w_edge, edge_gain, w_query, w_key, w_value, w_out
):
    rows, width = atoms.shape
    slots = neighbours.shape[1]
    devices = lax.axis_size("atom")
    reach = rows // 2
    levels = devices // 2

    def pp(x, f):
        return lax.ppermute(x, "atom", [(i, f(i)) for i in range(devices)])

    def up(x):
        return pp(x, lambda i: (i + 2) % devices)

    def down(x):
        return pp(x, lambda i: (i - 2) % devices)

    def flip(x):
        return pp(x, lambda i: i ^ 1)

    before = pp(atoms[rows - reach :], lambda i: (i + 1) % devices)
    after = pp(atoms[:reach], lambda i: (i - 1) % devices)
    base = lax.axis_index("atom") * rows - reach
    index_t = jnp.mod(neighbours - base, rows * devices).T
    slot_ids = jnp.arange(slots, dtype=jnp.int32)
    weight_t = jnp.where(slot_ids[None, :] < counts[:, None], envelope, jnp.float32(0.0)).T

    square = width * width * rows * 2
    self_t, other_own, edge_t = call(
        prep_kernel, (f32(width, rows), bf16(width, rows), bf16(width, width)), (), (2 * square, 0), "prep"
    )(atoms, w_self, w_other, w_edge)
    mixed = call(
        edge_kernel,
        bf16(rows, width),
        (pltpu.VMEM((width, 2 * rows), jnp.bfloat16), pltpu.VMEM((width, rows), jnp.float32)),
        (2 * slots * square, 2 * slots * rows * width),
        "edge",
    )(atoms, before, after, index_t, weight_t, self_t, other_own, w_other, edge_t, edge_gain[None, :])

    query, value_w = call(
        query_kernel, (bf16(HEADS, 2 * HEAD_DIM, rows), bf16(width, width)), (), (square, 0), "query"
    )(mixed, w_query, w_value)

    u, d = up(mixed), down(mixed)
    f = flip(mixed)
    carry = attend([mixed], query, w_key, value_w, None, None, "att0")
    arrived = [u, d]
    fu = fd = f
    pending = [f]
    hops = levels // 2
    for hop in range(1, hops + 1):
        batch = pending + arrived
        if hop < hops:
            u = up(u)
            arrived = [u]
            if hop + 1 < hops:
                d = down(d)
                arrived.append(d)
        else:
            arrived = []
        fd = down(fd)
        pending = [fd]
        if hop < hops:
            fu = up(fu)
            pending.append(fu)
        carry = attend(batch, query, w_key, value_w, carry, None, f"att{hop}")
    return attend(pending, query, w_key, value_w, carry, (mixed, w_out), "last")


def solution(mesh):
    rows = P(("sys", "atom"), None)
    return jax.shard_map(
        per_device,
        mesh=mesh,
        in_specs=(rows, rows, P(("sys", "atom")), rows) + (P(),) * 8,
        out_specs=rows,
        check_vma=False,
    )
```

```python
import functools
import math

import jax
import jax.numpy as jnp
from jax import lax
from jax.experimental import pallas as pl
from jax.experimental.pallas import tpu as pltpu
from jax.sharding import PartitionSpec as P

HEADS = 8
HEAD_DIM = 64

NT = (((1,), (1,)), ((), ()))
TN = (((0,), (0,)), ((), ()))


def mm(a, b, dims=(((1,), (0,)), ((), ()))):
    return lax.dot_general(a, b, dims, preferred_element_type=jnp.float32)


def silu(x):
    h = 0.5 * x
    return h + h * jnp.tanh(h)


def prep_kernel(
    own, w_self, w_other, w_edge, w_query, w_value, self_t, own_t, other_w, edge_t, query_w, value_w, buffer, sems
):
    copies = [
        pltpu.make_async_copy(w, buffer.at[i], sems.at[i])
        for i, w in enumerate((w_self, w_other, w_edge, w_query, w_value))
    ]
    for copy in copies:
        copy.start()
    copies[0].wait()
    self_t[...] = mm(buffer[0].T, own[...], NT)
    copies[1].wait()
    w_t = buffer[1].T
    other_w[...] = w_t
    own_t[...] = mm(w_t, own[...], NT).astype(jnp.bfloat16)
    for copy, i, out in zip(copies[2:], (2, 3, 4), (edge_t, query_w, value_w)):
        copy.wait()
        out[...] = buffer[i].T


def edge_kernel(own, before, after, idx_t, ew_t, self_t, own_t, other_w, edge_t, gain, mixed, table, acc, picked):
    rows = own.shape[0]
    half = rows // 2
    slots = idx_t.shape[0]
    span = 2 * rows
    table[:, :half] = mm(other_w[...], before[...], NT).astype(jnp.bfloat16)
    table[:, half : half + rows] = own_t[...]
    table[:, half + rows :] = mm(other_w[...], after[...], NT).astype(jnp.bfloat16)
    acc[...] = jnp.zeros_like(acc)

    def gather(k):
        hot = lax.broadcasted_iota(jnp.int32, (span, rows), 0) == idx_t[pl.ds(k, 1), :]
        return mm(table[...], jnp.where(hot, 1.0, 0.0).astype(jnp.bfloat16))

    def act(i):
        return silu(self_t[...] + picked[i]).astype(jnp.bfloat16)

    picked[0] = gather(0)
    picked[1] = gather(1)

    def step(j, carry):
        k = 2 * j
        first, second = act(0), act(1)
        picked[0] = gather(jnp.minimum(k + 2, slots - 2))
        even = mm(edge_t[...], first)
        picked[1] = gather(jnp.minimum(k + 3, slots - 1))
        odd = mm(edge_t[...], second)
        acc[...] += ew_t[pl.ds(k, 1), :] * silu(even) + ew_t[pl.ds(k + 1, 1), :] * silu(odd)
        return carry

    lax.fori_loop(0, slots // 2, step, 0)
    total = acc[...]
    mean_square = jnp.mean(total * total, axis=0, keepdims=True)
    normed = total * lax.rsqrt(mean_square + 1e-05)
    mixed[...] = (own[...].astype(jnp.float32) + gain[...] * normed.T).astype(jnp.bfloat16)


def query_kernel(own, query_w, query):
    scale = math.log2(math.e) / math.sqrt(HEAD_DIM)
    q_t = (mm(query_w[...], own[...], NT) * scale).astype(jnp.bfloat16)
    zero = jnp.zeros((HEAD_DIM, q_t.shape[1]), jnp.bfloat16)
    for h in range(HEADS):
        lo = h * HEAD_DIM
        mine = (h % 2) * HEAD_DIM
        query[h, mine : mine + HEAD_DIM, :] = q_t[lo : lo + HEAD_DIM]
        query[h, HEAD_DIM - mine : 2 * HEAD_DIM - mine, :] = zero


def attend_kernel(shards, first, last, *refs):
    xs, refs = refs[:shards], refs[shards:]
    query, w_key, value_w, refs = refs[0], refs[1], refs[2], refs[3:]
    if not first:
        state_in, sums_in, refs = refs[0], refs[1], refs[2:]
    if last:
        own, w_out, out, refs = refs[0], refs[1], refs[2], refs[3:]
    state, sums, stack, keys, values, scores = refs
    rows = xs[0].shape[0]
    for i, x in enumerate(xs):
        stack[i * rows : (i + 1) * rows, :] = x[...]
    keys[...] = mm(stack[...], w_key[...]).astype(jnp.bfloat16)
    values[...] = mm(value_w[...], stack[...], NT).astype(jnp.bfloat16)
    for h in range(HEADS):
        pair = (h // 2) * 2 * HEAD_DIM
        scores[h] = mm(keys[:, pair : pair + 2 * HEAD_DIM], query[h])
    for h in range(HEADS):
        mine = slice(h * HEAD_DIM, (h + 1) * HEAD_DIM)
        top = jnp.max(scores[h], axis=0, keepdims=True)
        if not first:
            old = sums_in[h : h + 1]
            top = jnp.maximum(old, top)
            factor = jnp.exp2(old - top)
        weights = jnp.exp2(scores[h] - top)
        total = jnp.sum(weights, axis=0, keepdims=True)
        product = mm(values[mine, :], weights.astype(jnp.bfloat16))
        if not first:
            total = factor * sums_in[HEADS + h : HEADS + h + 1] + total
            product = factor * state_in[mine, :] + product
        if last:
            state[mine, :] = product / total
        else:
            state[mine, :] = product
            sums[h : h + 1] = top
            sums[HEADS + h : HEADS + h + 1] = total
    if last:
        attended = state[...].T.astype(jnp.bfloat16)
        out[...] = (own[...].astype(jnp.float32) + mm(attended, w_out[...])).astype(jnp.bfloat16)


def call(body, out_shape, scratch=(), cost=None, name=None, in_specs=None):
    flops, trans = cost
    return pl.pallas_call(
        body,
        **({} if in_specs is None else {"in_specs": in_specs}),
        out_shape=out_shape,
        scratch_shapes=list(scratch),
        cost_estimate=pl.CostEstimate(flops=flops, transcendentals=trans, bytes_accessed=2**21),
        compiler_params=pltpu.CompilerParams(vmem_limit_bytes=40 * 2**20),
        name=name,
    )


def bf16(*shape):
    return jax.ShapeDtypeStruct(shape, jnp.bfloat16)


def f32(*shape):
    return jax.ShapeDtypeStruct(shape, jnp.float32)


def attend(xs, query, w_key, value_w, carry, tail, name):
    rows, width = xs[0].shape
    first, last = carry is None, tail is not None
    shards = len(xs)
    keys = shards * rows
    scratch = [
        pltpu.VMEM((keys, width), jnp.bfloat16),
        pltpu.VMEM((keys, width), jnp.bfloat16),
        pltpu.VMEM((width, keys), jnp.bfloat16),
        pltpu.VMEM((HEADS, keys, rows), jnp.float32),
    ]
    if last:
        out_shape = bf16(rows, width)
        scratch = [pltpu.VMEM((width, rows), jnp.float32), pltpu.VMEM((2 * HEADS, rows), jnp.float32)] + scratch
    else:
        out_shape = (f32(width, rows), f32(2 * HEADS, rows))
    cost = (shards * 4 * rows * width * width * 2, shards * HEADS * rows * rows)
    body = functools.partial(attend_kernel, shards, first, last)
    args = list(xs) + [query, w_key, value_w] + ([] if first else list(carry)) + (list(tail) if last else [])
    return call(body, out_shape, scratch, cost, name)(*args)


def per_device(
    atoms, neighbours, counts, envelope, w_self, w_other, w_edge, edge_gain, w_query, w_key, w_value, w_out
):
    rows, width = atoms.shape
    slots = neighbours.shape[1]
    devices = lax.axis_size("atom")
    reach = rows // 2

    def pp(x, f):
        return lax.ppermute(x, "atom", [(i, f(i)) for i in range(devices)])

    def up(x):
        return pp(x, lambda i: (i + 2) % devices)

    def down(x):
        return pp(x, lambda i: (i - 2) % devices)

    def flip(x):
        return pp(x, lambda i: i ^ 1)

    before = pp(atoms[rows - reach :], lambda i: (i + 1) % devices)
    after = pp(atoms[:reach], lambda i: (i - 1) % devices)
    base = lax.axis_index("atom") * rows - reach
    index_t = jnp.mod(neighbours - base, rows * devices).T
    slot_ids = jnp.arange(slots, dtype=jnp.int32)
    weight_t = jnp.where(slot_ids[None, :] < counts[:, None], envelope, jnp.float32(0.0)).T

    square = width * width * rows * 2
    vmem, hbm = pl.BlockSpec(memory_space=pltpu.VMEM), pl.BlockSpec(memory_space=pltpu.HBM)
    weight = bf16(width, width)
    self_t, own_t, other_w, edge_t, query_w, value_w = call(
        prep_kernel,
        (f32(width, rows), bf16(width, rows), weight, weight, weight, weight),
        (pltpu.VMEM((5, width, width), jnp.bfloat16), pltpu.SemaphoreType.DMA((5,))),
        (2 * square, 0),
        "prep",
        [vmem] + [hbm] * 5,
    )(atoms, w_self, w_other, w_edge, w_query, w_value)
    mixed = call(
        edge_kernel,
        bf16(rows, width),
        (
            pltpu.VMEM((width, 2 * rows), jnp.bfloat16),
            pltpu.VMEM((width, rows), jnp.float32),
            pltpu.VMEM((2, width, rows), jnp.float32),
        ),
        (2 * slots * square, 2 * slots * rows * width),
        "edge",
    )(atoms, before, after, index_t, weight_t, self_t, own_t, other_w, edge_t, edge_gain[None, :])

    barrier = lax.optimization_barrier
    u1, d1, f = up(mixed), down(mixed), flip(mixed)
    query = call(query_kernel, bf16(HEADS, 2 * HEAD_DIM, rows), (), (square, 0), "query")(mixed, query_w)
    tables = (query, w_key, value_w)
    carry = attend([mixed], *tables, None, None, "att0")
    u1, d1, f, carry = barrier((u1, d1, f, carry))
    u2, d2, p1 = up(u1), down(d1), flip(u1)
    carry = attend([u1, d1, f], *tables, carry, None, "att1")
    u2, d2, p1, carry = barrier((u2, d2, p1, carry))
    u3, d3, m1 = up(u2), down(d2), flip(d1)
    carry = attend([u2, d2, p1], *tables, carry, None, "att2")
    u3, d3, m1, carry = barrier((u3, d3, m1, carry))
    u4, m2, p2 = up(u3), down(m1), flip(u2)
    carry = attend([u3, d3, m1], *tables, carry, None, "att3")
    u4, m2, p2, carry = barrier((u4, m2, p2, carry))
    p3, m3, far = up(p2), down(m2), flip(u4)
    carry = attend([u4, m2, p2], *tables, carry, None, "att4")
    p3, m3, far, carry = barrier((p3, m3, far, carry))
    return attend([p3, m3, far], *tables, carry, (mixed, w_out), "last")


def solution(mesh):
    rows = P(("sys", "atom"), None)
    return jax.shard_map(
        per_device,
        mesh=mesh,
        in_specs=(rows, rows, P(("sys", "atom")), rows) + (P(),) * 8,
        out_specs=rows,
        check_vma=False,
    )
```

```python
import functools
import math

import jax
import jax.numpy as jnp
from jax import lax
from jax.experimental import pallas as pl
from jax.experimental.pallas import tpu as pltpu
from jax.sharding import PartitionSpec as P

HEADS = 8
HEAD_DIM = 64

NT = (((1,), (1,)), ((), ()))
TN = (((0,), (0,)), ((), ()))


def mm(a, b, dims=(((1,), (0,)), ((), ()))):
    return lax.dot_general(a, b, dims, preferred_element_type=jnp.float32)


def silu(x):
    h = 0.5 * x
    return h + h * jnp.tanh(h)


def prep_kernel(
    own, w_self, w_other, w_edge, w_query, w_value, self_t, own_t, other_w, edge_t, query_w, value_w, buffer, sems
):
    copies = [
        pltpu.make_async_copy(w, buffer.at[i], sems.at[i])
        for i, w in enumerate((w_self, w_other, w_edge, w_query, w_value))
    ]
    for copy in copies:
        copy.start()
    copies[0].wait()
    self_t[...] = mm(buffer[0].T, own[...], NT)
    copies[1].wait()
    w_t = buffer[1].T
    other_w[...] = w_t
    own_t[...] = mm(w_t, own[...], NT).astype(jnp.bfloat16)
    for copy, i, out in zip(copies[2:], (2, 3, 4), (edge_t, query_w, value_w)):
        copy.wait()
        out[...] = buffer[i].T


def edge_kernel(own, near, wide, idx_t, ew_t, self_t, own_t, other_w, edge_t, gain, mixed, table, acc, picked):
    rows = own.shape[0]
    half = rows // 2
    slots = idx_t.shape[0]
    span = 2 * rows
    table[:, :rows] = own_t[...]
    table[:, rows : rows + half] = mm(other_w[...], near[...], NT).astype(jnp.bfloat16)
    table[:, rows + half :] = mm(other_w[...], wide[...], NT).astype(jnp.bfloat16)
    acc[...] = jnp.zeros_like(acc)

    def gather(k):
        hot = lax.broadcasted_iota(jnp.int32, (span, rows), 0) == idx_t[pl.ds(k, 1), :]
        return mm(table[...], jnp.where(hot, 1.0, 0.0).astype(jnp.bfloat16))

    def act(i):
        return silu(self_t[...] + picked[i]).astype(jnp.bfloat16)

    picked[0] = gather(0)
    picked[1] = gather(1)

    def step(j, carry):
        k = 2 * j
        first, second = act(0), act(1)
        picked[0] = gather(jnp.minimum(k + 2, slots - 2))
        even = mm(edge_t[...], first)
        picked[1] = gather(jnp.minimum(k + 3, slots - 1))
        odd = mm(edge_t[...], second)
        acc[...] += ew_t[pl.ds(k, 1), :] * silu(even) + ew_t[pl.ds(k + 1, 1), :] * silu(odd)
        return carry

    lax.fori_loop(0, slots // 2, step, 0)
    total = acc[...]
    mean_square = jnp.mean(total * total, axis=0, keepdims=True)
    normed = total * lax.rsqrt(mean_square + 1e-05)
    mixed[...] = (own[...].astype(jnp.float32) + gain[...] * normed.T).astype(jnp.bfloat16)


def query_kernel(own, query_w, query):
    scale = math.log2(math.e) / math.sqrt(HEAD_DIM)
    q_t = (mm(query_w[...], own[...], NT) * scale).astype(jnp.bfloat16)
    zero = jnp.zeros((HEAD_DIM, q_t.shape[1]), jnp.bfloat16)
    for h in range(HEADS):
        lo = h * HEAD_DIM
        mine = (h % 2) * HEAD_DIM
        query[h, mine : mine + HEAD_DIM, :] = q_t[lo : lo + HEAD_DIM]
        query[h, HEAD_DIM - mine : 2 * HEAD_DIM - mine, :] = zero


def attend_kernel(shards, first, last, *refs):
    xs, refs = refs[:shards], refs[shards:]
    query, w_key, value_w, refs = refs[0], refs[1], refs[2], refs[3:]
    if not first:
        state_in, sums_in, refs = refs[0], refs[1], refs[2:]
    if last:
        own, w_out, out, refs = refs[0], refs[1], refs[2], refs[3:]
    state, sums, stack, keys, values, scores = refs
    rows = xs[0].shape[0]
    for i, x in enumerate(xs):
        stack[i * rows : (i + 1) * rows, :] = x[...]
    keys[...] = mm(stack[...], w_key[...]).astype(jnp.bfloat16)
    values[...] = mm(value_w[...], stack[...], NT).astype(jnp.bfloat16)
    for h in range(HEADS):
        pair = (h // 2) * 2 * HEAD_DIM
        scores[h] = mm(keys[:, pair : pair + 2 * HEAD_DIM], query[h])
    for h in range(HEADS):
        mine = slice(h * HEAD_DIM, (h + 1) * HEAD_DIM)
        top = jnp.max(scores[h], axis=0, keepdims=True)
        if not first:
            old = sums_in[h : h + 1]
            top = jnp.maximum(old, top)
            factor = jnp.exp2(old - top)
        weights = jnp.exp2(scores[h] - top)
        total = jnp.sum(weights, axis=0, keepdims=True)
        product = mm(values[mine, :], weights.astype(jnp.bfloat16))
        if not first:
            total = factor * sums_in[HEADS + h : HEADS + h + 1] + total
            product = factor * state_in[mine, :] + product
        if last:
            state[mine, :] = product / total
        else:
            state[mine, :] = product
            sums[h : h + 1] = top
            sums[HEADS + h : HEADS + h + 1] = total
    if last:
        attended = state[...].T.astype(jnp.bfloat16)
        out[...] = (own[...].astype(jnp.float32) + mm(attended, w_out[...])).astype(jnp.bfloat16)


def call(body, out_shape, scratch=(), cost=None, name=None, in_specs=None):
    flops, trans = cost
    return pl.pallas_call(
        body,
        **({} if in_specs is None else {"in_specs": in_specs}),
        out_shape=out_shape,
        scratch_shapes=list(scratch),
        cost_estimate=pl.CostEstimate(flops=flops, transcendentals=trans, bytes_accessed=2**21),
        compiler_params=pltpu.CompilerParams(vmem_limit_bytes=40 * 2**20),
        name=name,
    )


def bf16(*shape):
    return jax.ShapeDtypeStruct(shape, jnp.bfloat16)


def f32(*shape):
    return jax.ShapeDtypeStruct(shape, jnp.float32)


def attend(xs, query, w_key, value_w, carry, tail, name):
    rows, width = xs[0].shape
    first, last = carry is None, tail is not None
    shards = len(xs)
    keys = shards * rows
    scratch = [
        pltpu.VMEM((keys, width), jnp.bfloat16),
        pltpu.VMEM((keys, width), jnp.bfloat16),
        pltpu.VMEM((width, keys), jnp.bfloat16),
        pltpu.VMEM((HEADS, keys, rows), jnp.float32),
    ]
    if last:
        out_shape = bf16(rows, width)
        scratch = [pltpu.VMEM((width, rows), jnp.float32), pltpu.VMEM((2 * HEADS, rows), jnp.float32)] + scratch
    else:
        out_shape = (f32(width, rows), f32(2 * HEADS, rows))
    cost = (shards * 4 * rows * width * width * 2, shards * HEADS * rows * rows)
    body = functools.partial(attend_kernel, shards, first, last)
    args = list(xs) + [query, w_key, value_w] + ([] if first else list(carry)) + (list(tail) if last else [])
    return call(body, out_shape, scratch, cost, name)(*args)


def per_device(
    atoms, neighbours, counts, envelope, w_self, w_other, w_edge, edge_gain, w_query, w_key, w_value, w_out
):
    rows, width = atoms.shape
    slots = neighbours.shape[1]
    devices = lax.axis_size("atom")
    reach = rows // 2

    def pp(x, f):
        systems = lax.axis_size("sys")
        pairs = [
            (s * devices + i, s * devices + f(i, s % 2) % devices) for s in range(systems) for i in range(devices)
        ]
        return lax.ppermute(x, ("sys", "atom"), pairs)

    def up(x):
        return pp(x, lambda i, core: i + 2 - 4 * core)

    def down(x):
        return pp(x, lambda i, core: i - 2 + 4 * core)

    def flip(x):
        return pp(x, lambda i, core: i ^ 1)

    def halo(x, turn):
        return pp(x, lambda i, core: i ^ 1 if core == turn else i - 1 + 2 * (i % 2))

    place = lax.axis_index("atom")
    side = (place + lax.axis_index("sys")) % 2
    low, high = atoms[:reach], atoms[rows - reach :]
    even = side == 0
    near = halo(jnp.where(even, high, low), 0)
    wide = halo(jnp.where(even, low, high), 1)
    local = jnp.mod(neighbours - (place * rows - reach), rows * devices)
    after_first = jnp.where(even, 0, reach)
    before = local + rows + (reach - after_first)
    after = local - rows - reach + rows + after_first
    index_t = jnp.where(local < reach, before, jnp.where(local < rows + reach, local - reach, after)).T
    slot_ids = jnp.arange(slots, dtype=jnp.int32)
    weight_t = jnp.where(slot_ids[None, :] < counts[:, None], envelope, jnp.float32(0.0)).T

    square = width * width * rows * 2
    vmem, hbm = pl.BlockSpec(memory_space=pltpu.VMEM), pl.BlockSpec(memory_space=pltpu.HBM)
    weight = bf16(width, width)
    self_t, own_t, other_w, edge_t, query_w, value_w = call(
        prep_kernel,
        (f32(width, rows), bf16(width, rows), weight, weight, weight, weight),
        (pltpu.VMEM((5, width, width), jnp.bfloat16), pltpu.SemaphoreType.DMA((5,))),
        (2 * square, 0),
        "prep",
        [vmem] + [hbm] * 5,
    )(atoms, *[pltpu.with_memory_space_constraint(w, pltpu.HBM) for w in (w_self, w_other, w_edge, w_query, w_value)])
    mixed = call(
        edge_kernel,
        bf16(rows, width),
        (
            pltpu.VMEM((width, 2 * rows), jnp.bfloat16),
            pltpu.VMEM((width, rows), jnp.float32),
            pltpu.VMEM((2, width, rows), jnp.float32),
        ),
        (2 * slots * square, 2 * slots * rows * width),
        "edge",
    )(atoms, near, wide, index_t, weight_t, self_t, own_t, other_w, edge_t, edge_gain[None, :])

    barrier = lax.optimization_barrier
    u1, d1, f = up(mixed), down(mixed), flip(mixed)
    query = call(query_kernel, bf16(HEADS, 2 * HEAD_DIM, rows), (), (square, 0), "query")(mixed, query_w)
    tables = (query, w_key, value_w)
    carry = attend([mixed], *tables, None, None, "att0")
    u1, d1, f, carry = barrier((u1, d1, f, carry))
    u2, d2, p1 = up(u1), down(d1), flip(u1)
    carry = attend([u1, d1, f], *tables, carry, None, "att1")
    u2, d2, p1, carry = barrier((u2, d2, p1, carry))
    u3, d3, m1 = up(u2), down(d2), flip(d1)
    carry = attend([u2, d2, p1], *tables, carry, None, "att2")
    u3, d3, m1, carry = barrier((u3, d3, m1, carry))
    u4, m2, p2 = up(u3), down(m1), flip(u2)
    carry = attend([u3, d3, m1], *tables, carry, None, "att3")
    u4, m2, p2, carry = barrier((u4, m2, p2, carry))
    p3, m3, far = up(p2), down(m2), flip(u4)
    carry = attend([u4, m2, p2], *tables, carry, None, "att4")
    p3, m3, carry = barrier((p3, m3, carry))
    carry = attend([p3, m3], *tables, carry, None, "att5")
    return attend([far], *tables, carry, (mixed, w_out), "last")


def solution(mesh):
    rows = P(("sys", "atom"), None)
    return jax.shard_map(
        per_device,
        mesh=mesh,
        in_specs=(rows, rows, P(("sys", "atom")), rows) + (P(),) * 8,
        out_specs=rows,
        check_vma=False,
    )
```

```python
import functools
import math

import jax
import jax.numpy as jnp
from jax import lax
from jax.experimental import pallas as pl
from jax.experimental.pallas import tpu as pltpu
from jax.sharding import PartitionSpec as P

HEADS = 8
HEAD_DIM = 64

NT = (((1,), (1,)), ((), ()))
TN = (((0,), (0,)), ((), ()))


def mm(a, b, dims=(((1,), (0,)), ((), ()))):
    return lax.dot_general(a, b, dims, preferred_element_type=jnp.float32)


def silu(x):
    h = 0.5 * x
    return h + h * jnp.tanh(h)


def fetch(sources, buffer, sems):
    copies = [pltpu.make_async_copy(w, buffer.at[i], sems.at[i]) for i, w in enumerate(sources)]
    for copy in copies:
        copy.start()
    return copies


def prep_kernel(own, w_self, w_other, self_t, own_t, other_w, buffer, sems):
    copies = fetch((w_self, w_other), buffer, sems)
    copies[0].wait()
    self_t[...] = mm(buffer[0].T, own[...], NT)
    copies[1].wait()
    w_t = buffer[1].T
    other_w[...] = w_t
    own_t[...] = mm(w_t, own[...], NT).astype(jnp.bfloat16)


def turn_kernel(w_edge, w_query, w_value, after, edge_t, query_w, value_w, buffer, sems):
    copies = fetch((w_edge, w_query, w_value), buffer, sems)
    for i, out in enumerate((edge_t, query_w, value_w)):
        copies[i].wait()
        out[...] = buffer[i].T


def edge_kernel(own, near, wide, idx_t, ew_t, self_t, own_t, other_w, edge_t, gain, mixed, table, acc, picked):
    rows = own.shape[0]
    half = rows // 2
    slots = idx_t.shape[0]
    span = 2 * rows
    table[:, :rows] = own_t[...]
    table[:, rows : rows + half] = mm(other_w[...], near[...], NT).astype(jnp.bfloat16)
    table[:, rows + half :] = mm(other_w[...], wide[...], NT).astype(jnp.bfloat16)
    acc[...] = jnp.zeros_like(acc)

    def gather(k):
        hot = lax.broadcasted_iota(jnp.int32, (span, rows), 0) == idx_t[pl.ds(k, 1), :]
        return mm(table[...], jnp.where(hot, 1.0, 0.0).astype(jnp.bfloat16))

    def act(i):
        return silu(self_t[...] + picked[i]).astype(jnp.bfloat16)

    picked[0] = gather(0)
    picked[1] = gather(1)

    def step(j, carry):
        k = 2 * j
        first, second = act(0), act(1)
        picked[0] = gather(jnp.minimum(k + 2, slots - 2))
        even = mm(edge_t[...], first)
        picked[1] = gather(jnp.minimum(k + 3, slots - 1))
        odd = mm(edge_t[...], second)
        acc[...] += ew_t[pl.ds(k, 1), :] * silu(even) + ew_t[pl.ds(k + 1, 1), :] * silu(odd)
        return carry

    lax.fori_loop(0, slots // 2, step, 0)
    total = acc[...]
    mean_square = jnp.mean(total * total, axis=0, keepdims=True)
    normed = total * lax.rsqrt(mean_square + 1e-05)
    mixed[...] = (own[...].astype(jnp.float32) + gain[...] * normed.T).astype(jnp.bfloat16)


def query_kernel(own, query_w, query):
    scale = math.log2(math.e) / math.sqrt(HEAD_DIM)
    q_t = (mm(query_w[...], own[...], NT) * scale).astype(jnp.bfloat16)
    zero = jnp.zeros((HEAD_DIM, q_t.shape[1]), jnp.bfloat16)
    for h in range(HEADS):
        lo = h * HEAD_DIM
        mine = (h % 2) * HEAD_DIM
        query[h, mine : mine + HEAD_DIM, :] = q_t[lo : lo + HEAD_DIM]
        query[h, HEAD_DIM - mine : 2 * HEAD_DIM - mine, :] = zero


def project_kernel(x, w_key, value_w, keys, values):
    keys[...] = mm(x[...], w_key[...]).astype(jnp.bfloat16)
    values[...] = mm(value_w[...], x[...], NT).astype(jnp.bfloat16)


def attend_kernel(first, send, query, keys, values, *refs):
    if not first:
        state_in, sums_in, refs = refs[0], refs[1], refs[2:]
    if send:
        packed, sums, scores = refs
    else:
        state, sums, scores = refs
    for h in range(HEADS):
        pair = (h // 2) * 2 * HEAD_DIM
        scores[h] = mm(keys[:, pair : pair + 2 * HEAD_DIM], query[h])
    for h in range(HEADS):
        mine = slice(h * HEAD_DIM, (h + 1) * HEAD_DIM)
        top = jnp.max(scores[h], axis=0, keepdims=True)
        if not first:
            old = sums_in[h : h + 1]
            top = jnp.maximum(old, top)
            factor = jnp.exp2(old - top)
        weights = jnp.exp2(scores[h] - top)
        total = jnp.sum(weights, axis=0, keepdims=True)
        product = mm(values[mine, :], weights.astype(jnp.bfloat16))
        if not first:
            total = factor * sums_in[HEADS + h : HEADS + h + 1] + total
            product = factor * state_in[mine, :] + product
        if send:
            packed[mine, :] = (product / total).astype(jnp.bfloat16)
        else:
            state[mine, :] = product
        sums[h : h + 1] = top
        sums[HEADS + h : HEADS + h + 1] = total
    if send:
        height = sums[:HEADS] + jnp.log2(sums[HEADS:])
        high = height.astype(jnp.bfloat16).astype(jnp.float32)
        middle = (height - high).astype(jnp.bfloat16).astype(jnp.float32)
        pieces = [high, middle, height - high - middle, jnp.zeros_like(height)]
        packed[HEADS * HEAD_DIM :, :] = jnp.concatenate(pieces, axis=0).astype(jnp.bfloat16)


def finish_kernel(state, sums, packed, own, w_out, out, joined):
    depth = HEADS * HEAD_DIM
    extra = packed[depth:, :].astype(jnp.float32)
    other = extra[:HEADS] + extra[HEADS : 2 * HEADS] + extra[2 * HEADS : 3 * HEADS]
    mine = sums[:HEADS] + jnp.log2(sums[HEADS:])
    top = jnp.maximum(mine, other)
    left, right = jnp.exp2(mine - top), jnp.exp2(other - top)
    whole = left + right
    left, right = left / (whole * sums[HEADS:]), right / whole
    for h in range(HEADS):
        rows = slice(h * HEAD_DIM, (h + 1) * HEAD_DIM)
        theirs = packed[rows, :].astype(jnp.float32)
        joined[rows, :] = state[rows, :] * left[h : h + 1] + theirs * right[h : h + 1]
    attended = joined[...].T.astype(jnp.bfloat16)
    out[...] = (own[...].astype(jnp.float32) + mm(attended, w_out[...])).astype(jnp.bfloat16)


def call(body, out_shape, scratch=(), cost=None, name=None, in_specs=None):
    flops, trans = cost
    return pl.pallas_call(
        body,
        **({} if in_specs is None else {"in_specs": in_specs}),
        out_shape=out_shape,
        scratch_shapes=list(scratch),
        cost_estimate=pl.CostEstimate(flops=flops, transcendentals=trans, bytes_accessed=2**21),
        compiler_params=pltpu.CompilerParams(vmem_limit_bytes=40 * 2**20),
        name=name,
    )


def bf16(*shape):
    return jax.ShapeDtypeStruct(shape, jnp.bfloat16)


def f32(*shape):
    return jax.ShapeDtypeStruct(shape, jnp.float32)


def attend(query, table, carry, send, name):
    keys, values = table
    count, width = keys.shape
    rows = query.shape[2]
    first = carry is None
    main = bf16(width + 4 * HEADS, rows) if send else f32(width, rows)
    cost = (4 * count * rows * width, HEADS * count * rows)
    body = functools.partial(attend_kernel, first, send)
    scratch = (pltpu.VMEM((HEADS, count, rows), jnp.float32),)
    args = () if first else carry
    return call(body, (main, f32(2 * HEADS, rows)), scratch, cost, name)(query, keys, values, *args)


def per_device(
    atoms, neighbours, counts, envelope, w_self, w_other, w_edge, edge_gain, w_query, w_key, w_value, w_out
):
    rows, width = atoms.shape
    slots = neighbours.shape[1]
    devices = lax.axis_size("atom")
    reach = rows // 2

    def pp(x, f):
        systems = lax.axis_size("sys")
        pairs = [
            (s * devices + i, s * devices + f(i, s % 2) % devices) for s in range(systems) for i in range(devices)
        ]
        return lax.ppermute(x, ("sys", "atom"), pairs)

    def up(x):
        return pp(x, lambda i, core: i + 2 - 4 * core)

    def down(x):
        return pp(x, lambda i, core: i - 2 + 4 * core)

    def flip(x):
        return pp(x, lambda i, core: i ^ 1)

    def halo(x, turn):
        return pp(x, lambda i, core: i ^ 1 if core == turn else i - 1 + 2 * (i % 2))

    place = lax.axis_index("atom")
    side = (place + lax.axis_index("sys")) % 2
    low, high = atoms[:reach], atoms[rows - reach :]
    even = side == 0
    near = halo(jnp.where(even, high, low), 0)
    far_half = jnp.where(even, low, high)
    local = jnp.mod(neighbours - (place * rows - reach), rows * devices)
    after_first = jnp.where(even, 0, reach)
    before = local + rows + (reach - after_first)
    after = local - rows - reach + rows + after_first
    index_t = jnp.where(local < reach, before, jnp.where(local < rows + reach, local - reach, after)).T
    slot_ids = jnp.arange(slots, dtype=jnp.int32)
    weight_t = jnp.where(slot_ids[None, :] < counts[:, None], envelope, jnp.float32(0.0)).T

    square = width * width * rows * 2
    vmem, hbm = pl.BlockSpec(memory_space=pltpu.VMEM), pl.BlockSpec(memory_space=pltpu.HBM)
    weight = bf16(width, width)
    barrier = lax.optimization_barrier

    def in_hbm(*arrays):
        return [pltpu.with_memory_space_constraint(w, pltpu.HBM) for w in arrays]

    def fetched(count):
        return (pltpu.VMEM((count, width, width), jnp.bfloat16), pltpu.SemaphoreType.DMA((count,)))

    self_t, own_t, other_w = call(
        prep_kernel,
        (f32(width, rows), bf16(width, rows), weight),
        fetched(2),
        (2 * square, 0),
        "prep",
        [vmem] + [hbm] * 2,
    )(atoms, *in_hbm(w_self, w_other))
    far_half, self_t = barrier((far_half, self_t))
    wide = halo(far_half, 1)
    edge_t, query_w, value_w = call(
        turn_kernel, (weight,) * 3, fetched(3), (2**20, 0), "turn", [hbm] * 3 + [vmem]
    )(*in_hbm(w_edge, w_query, w_value), other_w)
    mixed = call(
        edge_kernel,
        bf16(rows, width),
        (
            pltpu.VMEM((width, 2 * rows), jnp.bfloat16),
            pltpu.VMEM((width, rows), jnp.float32),
            pltpu.VMEM((2, width, rows), jnp.float32),
        ),
        (2 * slots * square, 2 * slots * rows * width),
        "edge",
    )(atoms, near, wide, index_t, weight_t, self_t, own_t, other_w, edge_t, edge_gain[None, :])

    def ask(x, name):
        return call(query_kernel, bf16(HEADS, 2 * HEAD_DIM, rows), (), (square, 0), name)(x, query_w)

    def project(x, name):
        out = (bf16(rows, width), bf16(width, rows))
        return call(project_kernel, out, (), (2 * square, 0), name)(x, w_key, value_w)

    def both(x, mine, theirs, name):
        table = project(x, "kv_" + name)
        return attend(own_q, table, mine, False, "own_" + name), attend(pair_q, table, theirs, False, "pair_" + name)

    u, f = up(mixed), flip(mixed)
    own_q = ask(mixed, "ask_own")
    table = project(mixed, "kv_0")
    mine = attend(own_q, table, None, False, "own_0")
    own, mine = barrier((mixed, mine))
    d = down(own)
    f, mine = barrier((f, mine))
    pair_q = ask(f, "ask_pair")
    theirs = attend(pair_q, table, None, False, "pair_0")
    hops = devices // 4
    for hop in range(1, hops):
        u, mine, theirs = barrier((u, mine, theirs))
        held, u = u, up(u)
        mine, theirs = both(held, mine, theirs, f"u{hop}")
        d, mine, theirs = barrier((d, mine, theirs))
        held = d
        if hop + 1 < hops:
            d = down(d)
        mine, theirs = both(held, mine, theirs, f"d{hop}")
    u, mine, theirs = barrier((u, mine, theirs))
    table = project(u, "kv_last")
    packed, sums = attend(pair_q, table, theirs, True, "pair_last")
    returned = flip(packed)
    mine = attend(own_q, table, mine, False, "own_last")
    return call(
        finish_kernel, bf16(rows, width), (pltpu.VMEM((width, rows), jnp.float32),), (square, 0), "finish"
    )(*mine, returned, mixed, w_out)


def solution(mesh):
    rows = P(("sys", "atom"), None)
    return jax.shard_map(
        per_device,
        mesh=mesh,
        in_specs=(rows, rows, P(("sys", "atom")), rows) + (P(),) * 8,
        out_specs=rows,
        check_vma=False,
    )
```

```python
import functools
import math

import jax
import jax.numpy as jnp
from jax import lax
from jax.experimental import pallas as pl
from jax.experimental.pallas import tpu as pltpu
from jax.sharding import PartitionSpec as P

HEADS = 8
HEAD_DIM = 64

NT = (((1,), (1,)), ((), ()))
TN = (((0,), (0,)), ((), ()))


def mm(a, b, dims=(((1,), (0,)), ((), ()))):
    return lax.dot_general(a, b, dims, preferred_element_type=jnp.float32)


def silu(x):
    h = 0.5 * x
    return h + h * jnp.tanh(h)


def prep_kernel(
    own, near_by, envelope, counts, w_self, w_other, w_edge, w_query, w_value,
    self_t, own_s, own_t, other_w, edge_t, query_w, value_w, index_s, weight_s, count_s, order,
    near_buf, envelope_buf, count_buf, buffer, sems,
):
    rows = own.shape[0]
    half = rows // 2
    slots = near_buf.shape[0]
    sources = (counts, near_by, envelope, w_self, w_other, w_edge, w_query, w_value)
    targets = [count_buf, near_buf, envelope_buf] + [buffer.at[i] for i in range(5)]
    copies = [pltpu.make_async_copy(x, y, sems.at[i]) for i, (x, y) in enumerate(zip(sources, targets))]
    for copy in copies:
        copy.start()
    for copy in copies[:3]:
        copy.wait()
    f32, bf16 = jnp.float32, jnp.bfloat16
    count = count_buf[...].astype(f32)
    across = jnp.broadcast_to(count, (rows, rows))
    down = across.T
    earlier = lax.broadcasted_iota(jnp.int32, (rows, rows), 0) < lax.broadcasted_iota(jnp.int32, (rows, rows), 1)
    ahead = jnp.where(down > across, 1.0, jnp.where(down == across, jnp.where(earlier, 1.0, 0.0), 0.0))
    rank = jnp.sum(ahead, axis=0, keepdims=True)
    position = jnp.where(rank < half, rank, half + rows - 1 - rank).astype(jnp.int32)
    hot = lax.broadcasted_iota(jnp.int32, (rows, rows), 0) == position
    place_t = jnp.where(hot, 1.0, 0.0)
    order[...] = place_t.T.astype(bf16)
    move = place_t.astype(bf16)
    place = lax.axis_index("atom")
    even = (place + lax.axis_index("sys")) % 2 == 0
    system = rows * lax.axis_size("atom")
    local = near_buf[...] - (place * rows - half)
    local = jnp.where(local < 0, local + system, jnp.where(local >= system, local - system, local))
    shift = jnp.where(even, 0, half)
    below = local + rows + (half - shift)
    above = local - half + shift
    local = jnp.where(local < half, below, jnp.where(local < rows + half, local - half, above))
    weight = envelope_buf[...]
    high = weight.astype(bf16).astype(f32)
    middle = (weight - high).astype(bf16).astype(f32)
    low = weight - high - middle
    stack = [
        (local >> 4).astype(f32),
        (local & 15).astype(f32),
        high,
        middle,
        low,
        jnp.broadcast_to(count, (16, rows)),
    ]
    moved = mm(jnp.concatenate(stack, axis=0).astype(bf16), move, NT)
    index_s[...] = (moved[:slots] * 16.0 + moved[slots : 2 * slots]).astype(jnp.int32)
    weight_s[...] = moved[2 * slots : 3 * slots] + moved[3 * slots : 4 * slots] + moved[4 * slots : 5 * slots]
    count_s[...] = moved[5 * slots : 5 * slots + 8].astype(jnp.int32)
    ranked = mm(move, own[...]).astype(bf16)
    own_s[...] = ranked
    copies[3].wait()
    self_t[...] = mm(buffer[0].T, ranked, NT)
    copies[4].wait()
    w_t = buffer[1].T
    other_w[...] = w_t
    own_t[...] = mm(w_t, own[...], NT).astype(bf16)
    for i, out in ((2, edge_t), (3, query_w), (4, value_w)):
        copies[3 + i].wait()
        out[...] = buffer[i].T


def edge_kernel(
    own_s, near, wide, index_s, weight_s, count_s, self_t, own_t, other_w, edge_t, gain,
    mixed, table, self_two, acc, picked,
):
    rows = own_s.shape[0]
    half = rows // 2
    slots = index_s.shape[0]
    span = 2 * rows
    width = self_t.shape[0]
    table[:, :rows] = own_t[...]
    table[:, rows : rows + half] = mm(other_w[...], near[...], NT).astype(jnp.bfloat16)
    table[:, rows + half :] = mm(other_w[...], wide[...], NT).astype(jnp.bfloat16)
    for i in range(2):
        mine = self_t[:, i * half : (i + 1) * half]
        self_two[i, :, :half] = mine
        self_two[i, :, half:] = mine
    acc[...] = jnp.zeros_like(acc)
    front, back = count_s[0:1, :half], count_s[0:1, half:]
    steps = jnp.max(front + back)

    def lanes(s):
        r = steps - 1 - s
        a, b = jnp.minimum(s, slots - 1), jnp.clip(r, 0, slots - 1)
        in_front = s < front
        in_back = jnp.where(r < back, jnp.where(r >= 0, 1.0, 0.0), 0.0)
        index = jnp.where(in_front, index_s[pl.ds(a, 1), :][:, :half], index_s[pl.ds(b, 1), :][:, half:])
        ahead = jnp.where(in_front, weight_s[pl.ds(a, 1), :][:, :half], 0.0)
        behind = weight_s[pl.ds(b, 1), :][:, half:] * in_back
        return index, jnp.where(in_front, 1.0, 0.0), ahead, behind

    def unit(u):
        pieces = zip(lanes(2 * u), lanes(2 * u + 1))
        return [jnp.concatenate(pair, axis=1) for pair in pieces]

    def gather(u):
        index = unit(u)[0]
        hot = lax.broadcasted_iota(jnp.int32, (span, rows), 0) == index
        return mm(table[...], jnp.where(hot, 1.0, 0.0).astype(jnp.bfloat16))

    def act(i, u):
        chosen = jnp.broadcast_to(unit(u)[1], (width, rows)) > 0.5
        return silu(jnp.where(chosen, self_two[0], self_two[1]) + picked[i]).astype(jnp.bfloat16)

    def add(even, odd, u):
        for i in range(2):
            w_even, w_odd = unit(u)[2 + i], unit(u + 1)[2 + i]
            both = w_even * even + w_odd * odd
            acc[i] += both[:, :half] + both[:, half:]

    picked[0] = gather(0)
    picked[1] = gather(1)

    def step(j, carry):
        u = 2 * j
        first, second = act(0, u), act(1, u + 1)
        picked[0] = gather(u + 2)
        even = mm(edge_t[...], first)
        picked[1] = gather(u + 3)
        odd = mm(edge_t[...], second)
        add(silu(even), silu(odd), u)
        return carry

    lax.fori_loop(0, (steps + 3) // 4, step, 0)
    total = jnp.concatenate([acc[0], acc[1]], axis=1)
    mean_square = jnp.mean(total * total, axis=0, keepdims=True)
    normed = total * lax.rsqrt(mean_square + 1e-05)
    mixed[...] = (own_s[...].astype(jnp.float32) + gain[...] * normed.T).astype(jnp.bfloat16)


def query_kernel(own, query_w, query):
    scale = math.log2(math.e) / math.sqrt(HEAD_DIM)
    q_t = (mm(query_w[...], own[...], NT) * scale).astype(jnp.bfloat16)
    zero = jnp.zeros((HEAD_DIM, q_t.shape[1]), jnp.bfloat16)
    for h in range(HEADS):
        lo = h * HEAD_DIM
        mine = (h % 2) * HEAD_DIM
        query[h, mine : mine + HEAD_DIM, :] = q_t[lo : lo + HEAD_DIM]
        query[h, HEAD_DIM - mine : 2 * HEAD_DIM - mine, :] = zero


def project_kernel(x, w_key, value_w, keys, values):
    keys[...] = mm(x[...], w_key[...]).astype(jnp.bfloat16)
    values[...] = mm(value_w[...], x[...], NT).astype(jnp.bfloat16)


def attend_kernel(first, send, query, keys, values, *refs):
    if not first:
        state_in, sums_in, refs = refs[0], refs[1], refs[2:]
    if send:
        packed, sums, scores = refs
    else:
        state, sums, scores = refs
    for h in range(HEADS):
        pair = (h // 2) * 2 * HEAD_DIM
        scores[h] = mm(keys[:, pair : pair + 2 * HEAD_DIM], query[h])
    for h in range(HEADS):
        mine = slice(h * HEAD_DIM, (h + 1) * HEAD_DIM)
        top = jnp.max(scores[h], axis=0, keepdims=True)
        if not first:
            old = sums_in[h : h + 1]
            top = jnp.maximum(old, top)
            factor = jnp.exp2(old - top)
        weights = jnp.exp2(scores[h] - top)
        total = jnp.sum(weights, axis=0, keepdims=True)
        product = mm(values[mine, :], weights.astype(jnp.bfloat16))
        if not first:
            total = factor * sums_in[HEADS + h : HEADS + h + 1] + total
            product = factor * state_in[mine, :] + product
        if send:
            packed[mine, :] = (product / total).astype(jnp.bfloat16)
        else:
            state[mine, :] = product
        sums[h : h + 1] = top
        sums[HEADS + h : HEADS + h + 1] = total
    if send:
        height = sums[:HEADS] + jnp.log2(sums[HEADS:])
        high = height.astype(jnp.bfloat16).astype(jnp.float32)
        middle = (height - high).astype(jnp.bfloat16).astype(jnp.float32)
        pieces = [high, middle, height - high - middle, jnp.zeros_like(height)]
        packed[HEADS * HEAD_DIM :, :] = jnp.concatenate(pieces, axis=0).astype(jnp.bfloat16)


def finish_kernel(state, sums, packed, own, w_out, order, out, joined):
    depth = HEADS * HEAD_DIM
    extra = packed[depth:, :].astype(jnp.float32)
    other = extra[:HEADS] + extra[HEADS : 2 * HEADS] + extra[2 * HEADS : 3 * HEADS]
    mine = sums[:HEADS] + jnp.log2(sums[HEADS:])
    top = jnp.maximum(mine, other)
    left, right = jnp.exp2(mine - top), jnp.exp2(other - top)
    whole = left + right
    left, right = left / (whole * sums[HEADS:]), right / whole
    for h in range(HEADS):
        rows = slice(h * HEAD_DIM, (h + 1) * HEAD_DIM)
        theirs = packed[rows, :].astype(jnp.float32)
        joined[rows, :] = state[rows, :] * left[h : h + 1] + theirs * right[h : h + 1]
    attended = joined[...].T.astype(jnp.bfloat16)
    ranked = (own[...].astype(jnp.float32) + mm(attended, w_out[...])).astype(jnp.bfloat16)
    out[...] = mm(order[...], ranked).astype(jnp.bfloat16)


def call(body, out_shape, scratch=(), cost=None, name=None, in_specs=None):
    flops, trans = cost
    return pl.pallas_call(
        body,
        **({} if in_specs is None else {"in_specs": in_specs}),
        out_shape=out_shape,
        scratch_shapes=list(scratch),
        cost_estimate=pl.CostEstimate(flops=flops, transcendentals=trans, bytes_accessed=2**21),
        compiler_params=pltpu.CompilerParams(vmem_limit_bytes=40 * 2**20),
        name=name,
    )


def bf16(*shape):
    return jax.ShapeDtypeStruct(shape, jnp.bfloat16)


def f32(*shape):
    return jax.ShapeDtypeStruct(shape, jnp.float32)


def attend(query, table, carry, send, name):
    keys, values = table
    count, width = keys.shape
    rows = query.shape[2]
    first = carry is None
    main = bf16(width + 4 * HEADS, rows) if send else f32(width, rows)
    cost = (4 * count * rows * width, HEADS * count * rows)
    body = functools.partial(attend_kernel, first, send)
    scratch = (pltpu.VMEM((HEADS, count, rows), jnp.float32),)
    args = () if first else carry
    return call(body, (main, f32(2 * HEADS, rows)), scratch, cost, name)(query, keys, values, *args)


def per_device(
    atoms, neighbours, counts, envelope, w_self, w_other, w_edge, edge_gain, w_query, w_key, w_value, w_out
):
    rows, width = atoms.shape
    slots = neighbours.shape[1]
    devices = lax.axis_size("atom")
    reach = rows // 2

    def pp(x, f):
        systems = lax.axis_size("sys")
        pairs = [
            (s * devices + i, s * devices + f(i, s % 2) % devices) for s in range(systems) for i in range(devices)
        ]
        return lax.ppermute(x, ("sys", "atom"), pairs)

    def up(x):
        return pp(x, lambda i, core: i + 2 - 4 * core)

    def down(x):
        return pp(x, lambda i, core: i - 2 + 4 * core)

    def flip(x):
        return pp(x, lambda i, core: i ^ 1)

    def halo(x, turn):
        return pp(x, lambda i, core: i ^ 1 if core == turn else i - 1 + 2 * (i % 2))

    place = lax.axis_index("atom")
    side = (place + lax.axis_index("sys")) % 2
    low, high = atoms[:reach], atoms[rows - reach :]
    even = side == 0
    near = halo(jnp.where(even, high, low), 0)
    far_half = jnp.where(even, low, high)
    square = width * width * rows * 2
    vmem, hbm = pl.BlockSpec(memory_space=pltpu.VMEM), pl.BlockSpec(memory_space=pltpu.HBM)
    weight = bf16(width, width)
    barrier = lax.optimization_barrier

    def in_hbm(*arrays):
        return [pltpu.with_memory_space_constraint(w, pltpu.HBM) for w in arrays]

    listed = (neighbours.T, envelope.T, counts[None, :], w_self, w_other, w_edge, w_query, w_value)
    i32 = jax.ShapeDtypeStruct((slots, rows), jnp.int32)
    self_t, own_s, own_t, other_w, edge_t, query_w, value_w, index_s, weight_s, count_s, order = call(
        prep_kernel,
        (f32(width, rows), bf16(rows, width), bf16(width, rows), weight, weight, weight, weight)
        + (i32, f32(slots, rows), jax.ShapeDtypeStruct((8, rows), jnp.int32), bf16(rows, rows)),
        (
            pltpu.VMEM((slots, rows), jnp.int32),
            pltpu.VMEM((slots, rows), jnp.float32),
            pltpu.VMEM((1, rows), jnp.int32),
            pltpu.VMEM((5, width, width), jnp.bfloat16),
            pltpu.SemaphoreType.DMA((8,)),
        ),
        (2 * square, 0),
        "prep",
        [vmem] + [hbm] * 8,
    )(atoms, *in_hbm(*listed))
    far_half, self_t = barrier((far_half, self_t))
    wide = halo(far_half, 1)
    mixed = call(
        edge_kernel,
        bf16(rows, width),
        (
            pltpu.VMEM((width, 2 * rows), jnp.bfloat16),
            pltpu.VMEM((2, width, rows), jnp.float32),
            pltpu.VMEM((2, width, reach), jnp.float32),
            pltpu.VMEM((2, width, rows), jnp.float32),
        ),
        (slots * square, slots * rows * width),
        "edge",
    )(own_s, near, wide, index_s, weight_s, count_s, self_t, own_t, other_w, edge_t, edge_gain[None, :])

    def ask(x, name):
        return call(query_kernel, bf16(HEADS, 2 * HEAD_DIM, rows), (), (square, 0), name)(x, query_w)

    def project(x, name):
        out = (bf16(rows, width), bf16(width, rows))
        return call(project_kernel, out, (), (2 * square, 0), name)(x, w_key, value_w)

    def both(x, mine, theirs, name):
        table = project(x, "kv_" + name)
        return attend(own_q, table, mine, False, "own_" + name), attend(pair_q, table, theirs, False, "pair_" + name)

    u, f = up(mixed), flip(mixed)
    own_q = ask(mixed, "ask_own")
    table = project(mixed, "kv_0")
    mine = attend(own_q, table, None, False, "own_0")
    own, mine = barrier((mixed, mine))
    d = down(own)
    f, mine = barrier((f, mine))
    pair_q = ask(f, "ask_pair")
    theirs = attend(pair_q, table, None, False, "pair_0")
    hops = devices // 4
    for hop in range(1, hops):
        u, mine, theirs = barrier((u, mine, theirs))
        held, u = u, up(u)
        mine, theirs = both(held, mine, theirs, f"u{hop}")
        d, mine, theirs = barrier((d, mine, theirs))
        held = d
        if hop + 1 < hops:
            d = down(d)
        mine, theirs = both(held, mine, theirs, f"d{hop}")
    u, mine, theirs = barrier((u, mine, theirs))
    table = project(u, "kv_last")
    packed, sums = attend(pair_q, table, theirs, True, "pair_last")
    returned = flip(packed)
    mine = attend(own_q, table, mine, False, "own_last")
    return call(
        finish_kernel, bf16(rows, width), (pltpu.VMEM((width, rows), jnp.float32),), (square, 0), "finish"
    )(*mine, returned, mixed, w_out, order)


def solution(mesh):
    rows = P(("sys", "atom"), None)
    return jax.shard_map(
        per_device,
        mesh=mesh,
        in_specs=(rows, rows, P(("sys", "atom")), rows) + (P(),) * 8,
        out_specs=rows,
        check_vma=False,
    )
```
